32 devices in a mesh: rows: 16 (over z, x, core), cols: 2 (over y).
Axes of the slice: x: 2, y: 2, z: 4, core: 2. Of those that a mesh axis runs over, the one named last changes fastest.
Arguments:
- kernel: float32 [16384, 1536], P('rows', 'cols'), may hold values from -0.15625 to 0.15625
- row_orbitals: float32 [16384, 512], P('rows', 'cols'), may hold values from -1.5 to 1.5
- col_orbitals: float32 [1536, 512], P('cols', 'rows'), may hold values from -1.5 to 1.5
- col_vectors: float32 [1536, 512], P('cols', 'rows'), may hold values from -6 to 6
Outputs:
- exchange: float32 [512, 16384], P('cols', 'rows')
The draws below stay inside these ranges and needn't reach their ends.
All inputs are finite; a program needn't handle non-finite values.
Results may differ from the reference program's by a relative error of at most 0.0003.
Values sent between devices are 32-bit elements; how exact they have to be, the bound alone decides.
A program may use at most 64 MiB of HBM per device.

```python
import jax
import jax.numpy as jnp
from jax import lax

NORB = 512
ROW_DEV = 1024
ROWS = 16384
COLS = 1536


def block_levels(rng, dims, cuts, low, largest):
    loudness = 1.0
    for axis_at, parts in cuts:
        steps = jax.random.uniform(jax.random.fold_in(jax.random.fold_in(rng, 6), axis_at), (parts,), jnp.float32, low / len(cuts), largest / len(cuts))
        loudness = loudness * jnp.repeat(jnp.exp(steps), dims[axis_at] // parts).reshape((-1,) + (1,) * (len(dims) - 1 - axis_at))
    return loudness


def centred(rng, extent, width, most, pieces=(), held_as=jnp.bfloat16):
    gain = block_levels(rng, extent, pieces, -0.22, 0.18) if pieces else 1.0
    entries = jax.random.normal(rng, extent, jnp.float32) * width * gain
    return jnp.minimum(jnp.maximum(entries, -most), most).astype(held_as)


def setup_inputs(seed: int = 0) -> dict:
    arg_keys = jax.random.split(jax.random.key(seed), 5)
    kernel = centred(arg_keys[0], (ROWS, COLS), COLS ** -0.5, 0.15625, ((0, 16), (1, 2)), jnp.float32)
    row_orbitals = centred(arg_keys[1], (ROWS, NORB), 0.21, 1.5, ((0, 16), (1, 2)), jnp.float32)
    col_orbitals = centred(arg_keys[2], (COLS, NORB), 0.21, 1.5, ((0, 2), (1, 16)), jnp.float32)
    col_vectors = centred(arg_keys[3], (COLS, NORB), 1.0, 6.0, ((0, 2), (1, 16)), jnp.float32)
    return {"kernel": kernel, "row_orbitals": row_orbitals, "col_orbitals": col_orbitals, "col_vectors": col_vectors}


def reference(kernel, row_orbitals, col_orbitals, col_vectors):
    block_rows = min(1024, ROW_DEV)
    count = ROWS // block_rows

    def one_block(index):
        start = (index * block_rows).astype(jnp.int32)
        kernel_rows = lax.dynamic_slice_in_dim(kernel, start, block_rows, 0)
        orbs = lax.dynamic_slice_in_dim(row_orbitals, start, block_rows, 0)
        gram = jnp.dot(orbs, col_orbitals.T, precision=lax.Precision.HIGHEST, preferred_element_type=jnp.float32)
        weighted = kernel_rows * gram
        return -jnp.dot(col_vectors.T, weighted.T, precision=lax.Precision.HIGHEST, preferred_element_type=jnp.float32)

    blocks = lax.map(one_block, jnp.arange(count, dtype=jnp.int32))
    return jnp.transpose(blocks, (1, 0, 2)).reshape(NORB, ROWS)
```

```python
import functools

import jax
import jax.numpy as jnp
from jax import lax
from jax.experimental import pallas as pl
from jax.experimental.pallas import tpu as pltpu
from jax.sharding import PartitionSpec as P

MESH = pl.DeviceIdType.MESH
LEFT, RIGHT, PAIR, CORE = range(4)


def split(x):
    hi = x.astype(jnp.bfloat16)
    return hi, (x - hi.astype(jnp.float32)).astype(jnp.bfloat16)


def dot3(a_hi, a_lo, b_hi, b_lo, dims):
    dot = functools.partial(lax.dot_general, dimension_numbers=(dims, ((), ())), preferred_element_type=jnp.float32)
    return dot(a_lo, b_hi) + dot(a_hi, b_lo) + dot(a_hi, b_hi)


def exchange_kernel(
    nr, nc, chunks,
    k_hbm, row_hbm, orb_hbm, vec_hbm, out_ref,
    k, rows, orb, vec, orb_hi, orb_lo, vec_hi, vec_lo, theirs, got, mine,
    local_sem, ready, row_send, row_recv, col_send, col_recv, core_recv, out_send, out_recv,
):
    r, c = lax.axis_index("rows"), lax.axis_index("cols")
    core, chip = lax.rem(r, 2), r // 2
    pair, line, lines = lax.rem(chip, 2), chip // 2, nr // 4
    per = orb_hbm.shape[0]
    chunk = row_hbm.shape[0] // chunks
    mb = row_hbm.shape[1]
    nb = theirs.shape[2]

    def at(l, p, q):
        return (l * 2 + p) * 2 + q

    goal = {
        LEFT: at(line - 1, pair, core),
        RIGHT: at(line + 1, pair, core),
        PAIR: at(line, 1 - pair, core),
        CORE: at(line, pair, 1 - core),
    }
    has_left, has_right = line > 0, line < lines - 1

    barrier = pltpu.get_barrier_semaphore()

    def greet(row, col):
        pl.semaphore_signal(barrier, inc=1, device_id=(row, col), device_id_type=MESH)

    for j in range(1, nc):
        greet(r, lax.rem(c + j, nc))
    pl.when(core == 1)(lambda: greet(goal[CORE], c))
    pl.when(pair == 0)(lambda: greet(goal[PAIR], c))
    pl.when(has_right)(lambda: greet(goal[RIGHT], c))

    k_copy = pltpu.make_async_copy(k_hbm, k, local_sem.at[0])
    row_copy = pltpu.make_async_copy(row_hbm, rows.at[0], local_sem.at[1])
    own = pl.ds(pl.multiple_of(r * per, per), per)
    orb_copy = pltpu.make_async_copy(orb_hbm, orb.at[own], local_sem.at[2])
    vec_copy = pltpu.make_async_copy(vec_hbm, vec.at[own], local_sem.at[3])
    for copy in (k_copy, row_copy, orb_copy, vec_copy):
        copy.start()

    pl.semaphore_wait(barrier, nc - 1 + 1 - core + pair + has_left.astype(jnp.int32))

    def row_chunk(j, i):
        at_rows = pl.ds(i * chunk, chunk) if isinstance(i, int) else pl.ds(pl.multiple_of(i * chunk, chunk), chunk)
        return pltpu.make_async_remote_copy(
            src_ref=row_hbm.at[at_rows],
            dst_ref=rows.at[j, at_rows],
            send_sem=row_send.at[j - 1],
            recv_sem=row_recv.at[j - 1, i],
            device_id=(r, lax.rem(c + j, nc)),
            device_id_type=MESH,
        )

    for i in range(chunks):
        for j in range(1, nc):
            row_chunk(j, i).start()

    def answer(way, slot):
        pl.semaphore_signal(ready.at[slot], inc=1, device_id=(goal[way], c), device_id_type=MESH)

    pl.when(core == 0)(lambda: answer(CORE, CORE))
    pl.when(pair == 1)(lambda: answer(PAIR, PAIR))
    pl.when(has_left)(lambda: answer(LEFT, RIGHT))

    def shard(t, l, p, way, first=False):
        there = (orb, vec)[t].at[pl.ds(pl.multiple_of(at(l, p, core) * per, per), per)]
        return pltpu.make_async_remote_copy(
            src_ref=(orb_hbm, vec_hbm)[t] if first else there,
            dst_ref=there,
            send_sem=col_send.at[way],
            recv_sem=core_recv.at[0] if way == CORE else col_recv.at[t, p, l],
            device_id=(goal[way], c),
            device_id_type=MESH,
        )

    def line_sources(d):
        if d == 0:
            return [(line, None, ())]
        return [
            (line - d, line - d >= 0, ((RIGHT, has_right), (PAIR, None), (CORE, None))),
            (line + d, line + d < lines, ((LEFT, has_left), (PAIR, None), (CORE, None))),
        ]

    def when(cond, do):
        if cond is None:
            do()
        else:
            pl.when(cond)(do)

    def keep(t, s):
        here = pl.ds(pl.multiple_of(s * per, per), per)
        if t == 0:
            orb_hi[here], orb_lo[here] = split(orb[here])
        else:
            vec_hi[here], vec_lo[here] = split(-vec[here])

    def pass_on(t, d):
        for l, there, ways in line_sources(d):
            def go(l=l, ways=ways):
                shard(t, l, pair, PAIR).wait_recv()
                for way, cond in ways:
                    when(cond, shard(t, l, pair, way).start)
                keep(t, at(l, pair, core))
            when(there, go)

    def pass_over(t, d):
        for l, there, _ in line_sources(d):
            def go(l=l):
                shard(t, l, 1 - pair, PAIR).wait_recv()
                shard(t, l, 1 - pair, CORE).start()
                keep(t, at(l, 1 - pair, core))
            when(there, go)

    behind = ((CORE, core == 1), (PAIR, pair == 0), (RIGHT, has_right))
    for t in range(2):
        for way, cond in ((LEFT, has_left), (PAIR, pair == 1), (CORE, core == 0)):
            pl.when(cond)(shard(t, line, pair, way, True).start)
    for way, cond in behind:
        pl.when(cond)(lambda way=way: pl.semaphore_wait(ready.at[way], 1))
    for t in range(2):
        for way, cond in behind:
            pl.when(cond)(shard(t, line, pair, way, True).start)

    for d in range(lines):
        if d > 0:
            for t in range(2):
                pass_on(t, d)
        if d > 0:
            for t in range(2):
                pass_over(t, d - 1)
    for t in range(2):
        pass_over(t, lines - 1)

    def bulk(way, count):
        part = orb.at[pl.ds(0, count * per)]
        return pltpu.make_async_remote_copy(
            src_ref=part,
            dst_ref=part,
            send_sem=col_send.at[way],
            recv_sem=core_recv.at[0],
            device_id=(goal[CORE], c),
            device_id_type=MESH,
        )

    for copy in (orb_copy, vec_copy, k_copy, row_copy):
        copy.wait()
    for t in range(2):
        keep(t, r)
    bulk(CORE, nr).wait_recv()
    for t in range(2):

        @pl.loop(0, nr // 2)
        def _(m, t=t):
            keep(t, m * 2 + 1 - core)

    def out_chunk(j, i):
        return pltpu.make_async_remote_copy(
            src_ref=theirs.at[j - 1, i],
            dst_ref=got.at[j - 1, i],
            send_sem=out_send.at[j - 1],
            recv_sem=out_recv.at[j - 1, i],
            device_id=(r, lax.rem(c + j, nc)),
            device_id_type=MESH,
        )

    @pl.loop(0, chunks)
    def _(i):
        here = pl.ds(pl.multiple_of(i * chunk, chunk), chunk)
        gram = None
        for j in range(nc):
            if j > 0:
                row_chunk(j, i).wait_recv()
            block = pl.ds(pl.multiple_of(lax.rem(c - j + nc, nc) * mb, mb), mb)
            term = dot3(*split(rows[j, here, :]), orb_hi[block], orb_lo[block], ((1,), (0,)))
            gram = term if gram is None else gram + term
        w_hi, w_lo = split(k[here] * gram)
        for j in list(range(1, nc)) + [0]:
            block = pl.ds(pl.multiple_of(lax.rem(c + j, nc) * nb, nb), nb)
            part = dot3(vec_hi[block], vec_lo[block], w_hi, w_lo, ((1,), (1,)))
            if j == 0:
                mine[i] = part
            else:
                theirs[j - 1, i] = part
                out_chunk(j, i).start()

    bulk(PAIR, 2 * lines).wait_send()
    bulk(CORE, nr).wait_send()
    for l in range(lines):
        if l > 0:
            pl.when(line == l)(bulk(LEFT, 2 * (lines - l)).wait_send)
        if l < lines - 1:
            pl.when(line == l)(bulk(RIGHT, 2 * (l + 1)).wait_send)

    for i in range(chunks):
        total = mine[i]
        for j in range(1, nc):
            out_chunk(j, i).wait_recv()
            total = total + got[j - 1, i]
        out_ref[:, i * chunk:(i + 1) * chunk] = total
    for j in range(1, nc):
        peer = {"device_id": (r, lax.rem(c + j, nc)), "device_id_type": MESH}
        pltpu.make_async_remote_copy(
            row_hbm, rows.at[j], row_send.at[j - 1], row_recv.at[j - 1, 0], **peer
        ).wait_send()
        pltpu.make_async_remote_copy(
            theirs.at[j - 1], got.at[j - 1], out_send.at[j - 1], out_recv.at[j - 1, 0], **peer
        ).wait_send()


def solution(mesh):
    nr, nc = mesh.shape["rows"], mesh.shape["cols"]

    def body(kernel, row_orbitals, col_orbitals, col_vectors):
        n_rows, n_cols = kernel.shape
        mb, per = row_orbitals.shape[1], col_orbitals.shape[1]
        norb = mb * nc
        nb = norb // nc
        chunks = n_rows // 256
        chunk = n_rows // chunks
        f32, bf16, dma = jnp.float32, jnp.bfloat16, pltpu.SemaphoreType.DMA
        return pl.pallas_call(
            functools.partial(exchange_kernel, nr, nc, chunks),
            out_shape=pltpu.VMEM((nb, n_rows), f32),
            in_specs=[pl.BlockSpec(memory_space=pl.ANY)] * 4,
            out_specs=pl.BlockSpec(memory_space=pltpu.VMEM),
            scratch_shapes=[
                pltpu.VMEM((n_rows, n_cols), f32),
                pltpu.VMEM((nc, n_rows, mb), f32),
                pltpu.VMEM((norb, n_cols), f32),
                pltpu.VMEM((norb, n_cols), f32),
                pltpu.VMEM((norb, n_cols), bf16),
                pltpu.VMEM((norb, n_cols), bf16),
                pltpu.VMEM((norb, n_cols), bf16),
                pltpu.VMEM((norb, n_cols), bf16),
                pltpu.VMEM((nc - 1, chunks, nb, chunk), f32),
                pltpu.VMEM((nc - 1, chunks, nb, chunk), f32),
                pltpu.VMEM((chunks, nb, chunk), f32),
                dma((4,)),
                pltpu.SemaphoreType.REGULAR((4,)),
                dma((nc - 1,)),
                dma((nc - 1, chunks)),
                dma((4,)),
                dma((2, 2, nr // 4)),
                dma((1,)),
                dma((nc - 1,)),
                dma((nc - 1, chunks)),
            ],
            compiler_params=pltpu.CompilerParams(
                collective_id=0, has_side_effects=True, vmem_limit_bytes=60 * 1024 * 1024
            ),
        )(kernel, row_orbitals, col_orbitals.T, col_vectors.T)

    in_specs = (P("rows", "cols"), P("rows", "cols"), P("cols", "rows"), P("cols", "rows"))
    out_specs = P("cols", "rows")
    return jax.shard_map(body, mesh=mesh, in_specs=in_specs, out_specs=out_specs, check_vma=False)
```

```python
import functools

import jax
import jax.numpy as jnp
from jax import lax
from jax.experimental import pallas as pl
from jax.experimental.pallas import tpu as pltpu
from jax.sharding import PartitionSpec as P

MESH = pl.DeviceIdType.MESH
LEFT, RIGHT, PAIR, CORE = range(4)


def split(x):
    hi = x.astype(jnp.bfloat16)
    return hi, (x - hi.astype(jnp.float32)).astype(jnp.bfloat16)


def dot3(a_hi, a_lo, b_hi, b_lo, dims):
    dot = functools.partial(lax.dot_general, dimension_numbers=(dims, ((), ())), preferred_element_type=jnp.float32)
    return dot(a_lo, b_hi) + dot(a_hi, b_lo) + dot(a_hi, b_hi)


def exchange_kernel(
    nr, nc, chunks, pieces,
    k_hbm, row_hbm, orb_hbm, vec_hbm, out_ref,
    k, rows, orb, vec, orb_hi, orb_lo, vec_hi, vec_lo, w_hi, w_lo, theirs, got,
    local_sem, ready, row_send, row_recv, col_send, col_recv, core_recv, out_send, out_recv,
):
    r, c = lax.axis_index("rows"), lax.axis_index("cols")
    core, chip = lax.rem(r, 2), r // 2
    pair, line, lines = lax.rem(chip, 2), chip // 2, nr // 4
    per = orb_hbm.shape[0]
    chunk = row_hbm.shape[0] // chunks
    mb = row_hbm.shape[1]
    nb = theirs.shape[2]

    def at(l, p, q):
        return (l * 2 + p) * 2 + q

    goal = {
        LEFT: at(line - 1, pair, core),
        RIGHT: at(line + 1, pair, core),
        PAIR: at(line, 1 - pair, core),
        CORE: at(line, pair, 1 - core),
    }
    has_left, has_right = line > 0, line < lines - 1

    barrier = pltpu.get_barrier_semaphore()

    def greet(row, col):
        pl.semaphore_signal(barrier, inc=1, device_id=(row, col), device_id_type=MESH)

    for j in range(1, nc):
        greet(r, lax.rem(c + j, nc))
    pl.when(core == 1)(lambda: greet(goal[CORE], c))
    pl.when(pair == 0)(lambda: greet(goal[PAIR], c))
    pl.when(has_right)(lambda: greet(goal[RIGHT], c))

    k_copy = pltpu.make_async_copy(k_hbm, k, local_sem.at[0])
    row_copy = pltpu.make_async_copy(row_hbm, rows.at[0], local_sem.at[1])
    own = pl.ds(pl.multiple_of(r * per, per), per)
    orb_copy = pltpu.make_async_copy(orb_hbm, orb.at[own], local_sem.at[2])
    vec_copy = pltpu.make_async_copy(vec_hbm, vec.at[own], local_sem.at[3])
    for copy in (k_copy, row_copy, orb_copy, vec_copy):
        copy.start()

    pl.semaphore_wait(barrier, nc - 1 + 1 - core + pair + has_left.astype(jnp.int32))

    def row_chunk(j, i):
        at_rows = pl.ds(i * chunk, chunk) if isinstance(i, int) else pl.ds(pl.multiple_of(i * chunk, chunk), chunk)
        return pltpu.make_async_remote_copy(
            src_ref=row_hbm.at[at_rows],
            dst_ref=rows.at[j, at_rows],
            send_sem=row_send.at[j - 1],
            recv_sem=row_recv.at[j - 1, i],
            device_id=(r, lax.rem(c + j, nc)),
            device_id_type=MESH,
        )

    for i in range(chunks):
        for j in range(1, nc):
            row_chunk(j, i).start()

    def answer(way, slot):
        pl.semaphore_signal(ready.at[slot], inc=1, device_id=(goal[way], c), device_id_type=MESH)

    pl.when(core == 0)(lambda: answer(CORE, CORE))
    pl.when(pair == 1)(lambda: answer(PAIR, PAIR))
    pl.when(has_left)(lambda: answer(LEFT, RIGHT))

    split_by = pieces // 2
    part = per // split_by
    late_lines = lines // nc if lines % nc == 0 else 0

    def late(l):
        return l // late_lines == c if late_lines else l < 0

    def at_piece(q, s):
        return pl.ds(pl.multiple_of(s * per + q % split_by * part, part), part)

    def shard(q, l, p, way, first=False):
        t = q // split_by
        there = (orb, vec)[t].at[at_piece(q, at(l, p, core))]
        return pltpu.make_async_remote_copy(
            src_ref=(orb_hbm, vec_hbm)[t].at[pl.ds(q % split_by * part, part)] if first else there,
            dst_ref=there,
            send_sem=col_send.at[way],
            recv_sem=core_recv.at[phase_of(q, l)] if way == CORE else col_recv.at[q, p, l],
            device_id=(goal[way], c),
            device_id_type=MESH,
        )

    def phase_of(q, l):
        return 0 if q < split_by else late(l).astype(jnp.int32)

    def line_sources(d):
        if d == 0:
            return [(line, None, ())]
        return [
            (line - d, line - d >= 0, ((RIGHT, has_right), (PAIR, None), (CORE, None))),
            (line + d, line + d < lines, ((LEFT, has_left), (PAIR, None), (CORE, None))),
        ]

    def both(a, b):
        return b if a is None else a if b is None else a & b

    def when(cond, do):
        if cond is None:
            do()
        else:
            pl.when(cond)(do)

    def keep(t, rows_here):
        if t == 0:
            orb_hi[rows_here], orb_lo[rows_here] = split(orb[rows_here])
        else:
            vec_hi[rows_here], vec_lo[rows_here] = split(-vec[rows_here])

    def whole(s):
        return pl.ds(pl.multiple_of(s * per, per), per)

    def now(q, l, second):
        if q < split_by:
            return None
        return late(l) if second else ~late(l)

    def pass_on(q, d, second):
        for l, there, ways in line_sources(d):
            def go(l=l, ways=ways):
                shard(q, l, pair, PAIR).wait_recv()
                for way, cond in ways:
                    when(cond, shard(q, l, pair, way).start)
                keep(q // split_by, at_piece(q, at(l, pair, core)))
            when(both(there, now(q, l, second)), go)

    def pass_over(q, d, second):
        for l, there, _ in line_sources(d):
            def go(l=l):
                shard(q, l, 1 - pair, PAIR).wait_recv()
                shard(q, l, 1 - pair, CORE).start()
                keep(q // split_by, at_piece(q, at(l, 1 - pair, core)))
            when(both(there, now(q, l, second)), go)

    def gather(some, second):
        for d in range(1, lines):
            for q in some:
                pass_on(q, d, second)
            for q in some:
                pass_over(q, d - 1, second)
        for q in some:
            pass_over(q, lines - 1, second)

    ahead = ((LEFT, has_left), (PAIR, pair == 1), (CORE, core == 0))
    behind = ((CORE, core == 1), (PAIR, pair == 0), (RIGHT, has_right))
    for q in range(pieces):
        for way, cond in ahead:
            when(both(cond, now(q, line, False)), shard(q, line, pair, way, True).start)
    for way, cond in behind:
        pl.when(cond)(lambda way=way: pl.semaphore_wait(ready.at[way], 1))
    for q in range(pieces):
        for way, cond in behind:
            when(both(cond, now(q, line, False)), shard(q, line, pair, way, True).start)

    gather(range(pieces), False)

    def bulk(way, count, phase=0):
        some = orb.at[pl.ds(0, count * per)]
        return pltpu.make_async_remote_copy(
            src_ref=some,
            dst_ref=some,
            send_sem=col_send.at[way],
            recv_sem=core_recv.at[phase],
            device_id=(goal[CORE], c),
            device_id_type=MESH,
        )

    for copy in (orb_copy, vec_copy, k_copy, row_copy):
        copy.wait()
    for t in range(2):
        keep(t, whole(r))
    bulk(CORE, nr - 2 * late_lines).wait_recv()

    @pl.loop(0, nr // 2)
    def _(m):
        keep(0, whole(m * 2 + 1 - core))

    @pl.loop(0, nr // 2 - 2 * late_lines)
    def _(m):
        m = m + jnp.where(m >= c * 2 * late_lines, 2 * late_lines, 0)
        keep(1, whole(m * 2 + 1 - core))

    def out_chunk(j, i):
        return pltpu.make_async_remote_copy(
            src_ref=theirs.at[j - 1, i],
            dst_ref=got.at[j - 1, i],
            send_sem=out_send.at[j - 1],
            recv_sem=out_recv.at[j - 1, i],
            device_id=(r, lax.rem(c + j, nc)),
            device_id_type=MESH,
        )

    def partial(j, here):
        block = pl.ds(pl.multiple_of(lax.rem(c + j, nc) * nb, nb), nb)
        return dot3(vec_hi[block], vec_lo[block], w_hi[here], w_lo[here], ((1,), (1,)))

    @pl.loop(0, chunks)
    def _(i):
        here = pl.ds(pl.multiple_of(i * chunk, chunk), chunk)
        gram = None
        for j in range(nc):
            if j > 0:
                row_chunk(j, i).wait_recv()
            block = pl.ds(pl.multiple_of(lax.rem(c - j + nc, nc) * mb, mb), mb)
            term = dot3(*split(rows[j, here, :]), orb_hi[block], orb_lo[block], ((1,), (0,)))
            gram = term if gram is None else gram + term
        w_hi[here], w_lo[here] = split(k[here] * gram)
        for j in range(1, nc):
            theirs[j - 1, i] = partial(j, here)
            out_chunk(j, i).start()

    if late_lines:
        for way, cond in ahead + behind:
            for q in range(split_by, pieces):
                pl.when(cond & late(line))(shard(q, line, pair, way, True).start)
        gather(range(split_by, pieces), True)
        bulk(CORE, 2 * late_lines, 1).wait_recv()

        @pl.loop(0, 2 * late_lines)
        def _(m):
            keep(1, whole((c * 2 * late_lines + m) * 2 + 1 - core))

    @pl.loop(0, chunks)
    def _(i):
        here = pl.ds(pl.multiple_of(i * chunk, chunk), chunk)
        out_ref[:, here] = partial(0, here)

    bulk(PAIR, 2 * lines).wait_send()
    bulk(CORE, nr).wait_send()
    for l in range(lines):
        if l > 0:
            pl.when(line == l)(bulk(LEFT, 2 * (lines - l)).wait_send)
        if l < lines - 1:
            pl.when(line == l)(bulk(RIGHT, 2 * (l + 1)).wait_send)

    for i in range(chunks):
        here = pl.ds(i * chunk, chunk)
        total = out_ref[:, here]
        for j in range(1, nc):
            out_chunk(j, i).wait_recv()
            total = total + got[j - 1, i]
        out_ref[:, here] = total
    for j in range(1, nc):
        peer = {"device_id": (r, lax.rem(c + j, nc)), "device_id_type": MESH}
        pltpu.make_async_remote_copy(
            row_hbm, rows.at[j], row_send.at[j - 1], row_recv.at[j - 1, 0], **peer
        ).wait_send()
        pltpu.make_async_remote_copy(
            theirs.at[j - 1], got.at[j - 1], out_send.at[j - 1], out_recv.at[j - 1, 0], **peer
        ).wait_send()


def solution(mesh):
    nr, nc = mesh.shape["rows"], mesh.shape["cols"]

    def body(kernel, row_orbitals, col_orbitals, col_vectors):
        n_rows, n_cols = kernel.shape
        mb, per = row_orbitals.shape[1], col_orbitals.shape[1]
        norb = mb * nc
        nb = norb // nc
        chunks = n_rows // 256
        chunk = n_rows // chunks
        pieces = 4 if per % 32 == 0 else 2
        f32, bf16, dma = jnp.float32, jnp.bfloat16, pltpu.SemaphoreType.DMA
        return pl.pallas_call(
            functools.partial(exchange_kernel, nr, nc, chunks, pieces),
            out_shape=pltpu.VMEM((nb, n_rows), f32),
            in_specs=[pl.BlockSpec(memory_space=pl.ANY)] * 4,
            out_specs=pl.BlockSpec(memory_space=pltpu.VMEM),
            scratch_shapes=[
                pltpu.VMEM((n_rows, n_cols), f32),
                pltpu.VMEM((nc, n_rows, mb), f32),
                pltpu.VMEM((norb, n_cols), f32),
                pltpu.VMEM((norb, n_cols), f32),
                pltpu.VMEM((norb, n_cols), bf16),
                pltpu.VMEM((norb, n_cols), bf16),
                pltpu.VMEM((norb, n_cols), bf16),
                pltpu.VMEM((norb, n_cols), bf16),
                pltpu.VMEM((n_rows, n_cols), bf16),
                pltpu.VMEM((n_rows, n_cols), bf16),
                pltpu.VMEM((nc - 1, chunks, nb, chunk), f32),
                pltpu.VMEM((nc - 1, chunks, nb, chunk), f32),
                dma((4,)),
                pltpu.SemaphoreType.REGULAR((4,)),
                dma((nc - 1,)),
                dma((nc - 1, chunks)),
                dma((4,)),
                dma((pieces, 2, nr // 4)),
                dma((2,)),
                dma((nc - 1,)),
                dma((nc - 1, chunks)),
            ],
            compiler_params=pltpu.CompilerParams(
                collective_id=0, has_side_effects=True, vmem_limit_bytes=60 * 1024 * 1024
            ),
        )(kernel, row_orbitals, col_orbitals.T, col_vectors.T)

    in_specs = (P("rows", "cols"), P("rows", "cols"), P("cols", "rows"), P("cols", "rows"))
    out_specs = P("cols", "rows")
    return jax.shard_map(body, mesh=mesh, in_specs=in_specs, out_specs=out_specs, check_vma=False)
```

```python
import functools

import jax
import jax.numpy as jnp
from jax import lax
from jax.experimental import pallas as pl
from jax.experimental.pallas import tpu as pltpu
from jax.sharding import PartitionSpec as P

MESH = pl.DeviceIdType.MESH
LEFT, RIGHT, PAIR, CORE = range(4)


def split(x):
    hi = x.astype(jnp.bfloat16)
    return hi, (x - hi.astype(jnp.float32)).astype(jnp.bfloat16)


def dot3(a_hi, a_lo, b_hi, b_lo, dims):
    dot = functools.partial(lax.dot_general, dimension_numbers=(dims, ((), ())), preferred_element_type=jnp.float32)
    return dot(a_lo, b_hi) + dot(a_hi, b_lo) + dot(a_hi, b_hi)


def exchange_kernel(
    nr, nc, chunks, pieces, detour,
    k_hbm, row_hbm, orb_hbm, vec_hbm, out_ref,
    k, rows, orb, vec, orb_hi, orb_lo, vec_hi, vec_lo, w_hi, w_lo, theirs, got, relay,
    local_sem, ready, row_send, row_recv, col_send, col_recv, core_recv, out_send, out_recv, relay_send, relay_recv,
):
    r, c = lax.axis_index("rows"), lax.axis_index("cols")
    core, chip = lax.rem(r, 2), r // 2
    pair, line, lines = lax.rem(chip, 2), chip // 2, nr // 4
    per = orb_hbm.shape[0]
    chunk = row_hbm.shape[0] // chunks
    mb = row_hbm.shape[1]
    nb = theirs.shape[2]

    def at(l, p, q):
        return (l * 2 + p) * 2 + q

    goal = {
        LEFT: at(line - 1, pair, core),
        RIGHT: at(line + 1, pair, core),
        PAIR: at(line, 1 - pair, core),
        CORE: at(line, pair, 1 - core),
    }
    has_left, has_right = line > 0, line < lines - 1

    barrier = pltpu.get_barrier_semaphore()

    def greet(row, col):
        pl.semaphore_signal(barrier, inc=1, device_id=(row, col), device_id_type=MESH)

    for j in range(1, nc):
        greet(r, lax.rem(c + j, nc))
    pl.when(core == 1)(lambda: greet(goal[CORE], c))
    pl.when(pair == 0)(lambda: greet(goal[PAIR], c))
    pl.when(has_right)(lambda: greet(goal[RIGHT], c))

    k_copy = pltpu.make_async_copy(k_hbm, k, local_sem.at[0])
    row_copy = pltpu.make_async_copy(row_hbm, rows.at[0], local_sem.at[1])
    own = pl.ds(pl.multiple_of(r * per, per), per)
    orb_copy = pltpu.make_async_copy(orb_hbm, orb.at[own], local_sem.at[2])
    vec_copy = pltpu.make_async_copy(vec_hbm, vec.at[own], local_sem.at[3])

    pl.semaphore_wait(barrier, nc - 1 + 1 - core + pair + has_left.astype(jnp.int32))

    def row_chunk(j, i, size=chunk):
        at_rows = pl.ds(i * chunk if isinstance(i, int) else pl.multiple_of(i * chunk, chunk), size)
        return pltpu.make_async_remote_copy(
            src_ref=row_hbm.at[at_rows],
            dst_ref=rows.at[j, at_rows],
            send_sem=row_send.at[j - 1],
            recv_sem=row_recv.at[j - 1, i],
            device_id=(r, lax.rem(c + j, nc)),
            device_id_type=MESH,
        )

    to_first = (r == 0) & (c == 1)
    helps = [(at(0, 1, 0), PAIR), (at(1, 0, 0), RIGHT)] if detour else []
    direct = chunk - len(helps) * detour

    def row_tail(h, device, src=row_hbm, dst=rows, send=None, recv=None):
        there = pl.ds((chunks - 1) * chunk + direct + h * detour, detour)
        return pltpu.make_async_remote_copy(
            src_ref=relay if src is relay else src.at[there],
            dst_ref=relay if dst is relay else dst.at[1, there],
            send_sem=send,
            recv_sem=recv,
            device_id=device,
            device_id_type=MESH,
        )

    for i in range(chunks):
        for j in range(1, nc):
            if helps and i == chunks - 1:
                pl.when(~to_first)(row_chunk(j, i).start)
                pl.when(to_first)(row_chunk(j, i, direct).start)
            else:
                row_chunk(j, i).start()

    def answer(way, slot):
        pl.semaphore_signal(ready.at[slot], inc=1, device_id=(goal[way], c), device_id_type=MESH)

    pl.when(core == 0)(lambda: answer(CORE, CORE))
    pl.when(pair == 1)(lambda: answer(PAIR, PAIR))
    pl.when(has_left)(lambda: answer(LEFT, RIGHT))

    split_by = pieces // 2
    part = per // split_by
    late_lines = lines // nc if lines % nc == 0 else 0

    def late(l):
        return l // late_lines == c if late_lines else l < 0

    def at_piece(q, s):
        return pl.ds(pl.multiple_of(s * per + q % split_by * part, part), part)

    def shard(q, l, p, way, first=False):
        t = q // split_by
        there = (orb, vec)[t].at[at_piece(q, at(l, p, core))]
        return pltpu.make_async_remote_copy(
            src_ref=(orb_hbm, vec_hbm)[t].at[pl.ds(q % split_by * part, part)] if first else there,
            dst_ref=there,
            send_sem=col_send.at[way],
            recv_sem=core_recv.at[phase_of(q, l)] if way == CORE else col_recv.at[q, p, l],
            device_id=(goal[way], c),
            device_id_type=MESH,
        )

    def phase_of(q, l):
        return 0 if q < split_by else late(l).astype(jnp.int32)

    def line_sources(d):
        if d == 0:
            return [(line, None, ())]
        return [
            (line - d, line - d >= 0, ((RIGHT, has_right), (PAIR, None), (CORE, None))),
            (line + d, line + d < lines, ((LEFT, has_left), (PAIR, None), (CORE, None))),
        ]

    def both(a, b):
        return b if a is None else a if b is None else a & b

    def when(cond, do):
        if cond is None:
            do()
        else:
            pl.when(cond)(do)

    def keep(t, rows_here):
        if t == 0:
            orb_hi[rows_here], orb_lo[rows_here] = split(orb[rows_here])
        else:
            vec_hi[rows_here], vec_lo[rows_here] = split(-vec[rows_here])

    def whole(s):
        return pl.ds(pl.multiple_of(s * per, per), per)

    def now(q, l, second):
        if q < split_by:
            return None
        return late(l) if second else ~late(l)

    def pass_on(q, d, second):
        for l, there, ways in line_sources(d):
            def go(l=l, ways=ways):
                shard(q, l, pair, PAIR).wait_recv()
                for way, cond in ways:
                    when(cond, shard(q, l, pair, way).start)
                keep(q // split_by, at_piece(q, at(l, pair, core)))
            when(both(there, now(q, l, second)), go)

    def pass_over(q, d, second):
        for l, there, _ in line_sources(d):
            def go(l=l):
                shard(q, l, 1 - pair, PAIR).wait_recv()
                shard(q, l, 1 - pair, CORE).start()
                keep(q // split_by, at_piece(q, at(l, 1 - pair, core)))
            when(both(there, now(q, l, second)), go)

    def gather(some, second):
        for d in range(1, lines):
            for q in some:
                pass_on(q, d, second)
            for q in some:
                pass_over(q, d - 1, second)
        for q in some:
            pass_over(q, lines - 1, second)

    ahead = ((LEFT, has_left), (PAIR, pair == 1), (CORE, core == 0))
    behind = ((CORE, core == 1), (PAIR, pair == 0), (RIGHT, has_right))
    for q in range(pieces):
        for way, cond in ahead:
            when(both(cond, now(q, line, False)), shard(q, line, pair, way, True).start)
    for way, cond in behind:
        pl.when(cond)(lambda way=way: pl.semaphore_wait(ready.at[way], 1))
    for q in range(pieces):
        for way, cond in behind:
            when(both(cond, now(q, line, False)), shard(q, line, pair, way, True).start)

    for h, (_, way) in enumerate(helps):
        pl.when(to_first)(row_tail(h, (goal[way], c), row_hbm, relay, row_send.at[0], relay_recv.at[0]).start)
    for h, (helper, _) in enumerate(helps):

        @pl.when((r == helper) & (c == 1))
        def _(h=h):
            row_tail(h, (r, 0), row_hbm, relay, relay_send.at[0], relay_recv.at[0]).wait_recv()
            row_tail(h, (r, 0), relay, relay, relay_send.at[0], relay_recv.at[0]).start()

    for copy in (k_copy, row_copy, orb_copy, vec_copy):
        copy.start()

    gather(range(pieces), False)

    def bulk(way, count, phase=0):
        some = orb.at[pl.ds(0, count * per)]
        return pltpu.make_async_remote_copy(
            src_ref=some,
            dst_ref=some,
            send_sem=col_send.at[way],
            recv_sem=core_recv.at[phase],
            device_id=(goal[CORE], c),
            device_id_type=MESH,
        )

    for copy in (orb_copy, vec_copy, k_copy, row_copy):
        copy.wait()
    for t in range(2):
        keep(t, whole(r))
    bulk(CORE, nr - 2 * late_lines).wait_recv()

    @pl.loop(0, nr // 2)
    def _(m):
        keep(0, whole(m * 2 + 1 - core))

    @pl.loop(0, nr // 2 - 2 * late_lines)
    def _(m):
        m = m + jnp.where(m >= c * 2 * late_lines, 2 * late_lines, 0)
        keep(1, whole(m * 2 + 1 - core))

    def out_chunk(j, i):
        return pltpu.make_async_remote_copy(
            src_ref=theirs.at[j - 1, i],
            dst_ref=got.at[j - 1, i],
            send_sem=out_send.at[j - 1],
            recv_sem=out_recv.at[j - 1, i],
            device_id=(r, lax.rem(c + j, nc)),
            device_id_type=MESH,
        )

    def partial(j, here):
        block = pl.ds(pl.multiple_of(lax.rem(c + j, nc) * nb, nb), nb)
        return dot3(vec_hi[block], vec_lo[block], w_hi[here], w_lo[here], ((1,), (1,)))

    @pl.loop(0, chunks)
    def _(i):
        here = pl.ds(pl.multiple_of(i * chunk, chunk), chunk)
        gram = None
        for j in range(nc):
            if j > 0:
                row_chunk(j, i).wait_recv()
            block = pl.ds(pl.multiple_of(lax.rem(c - j + nc, nc) * mb, mb), mb)
            term = dot3(*split(rows[j, here, :]), orb_hi[block], orb_lo[block], ((1,), (0,)))
            gram = term if gram is None else gram + term
        w_hi[here], w_lo[here] = split(k[here] * gram)
        for j in range(1, nc):
            theirs[j - 1, i] = partial(j, here)
            out_chunk(j, i).start()

    for h, (helper, _) in enumerate(helps):

        @pl.when((r == helper) & (c == 0))
        def _(h=h):
            row_tail(h, (r, 0), row_hbm, relay, relay_send.at[0], relay_recv.at[0]).wait_recv()
            row_tail(h, (0, 0), relay, rows, relay_send.at[0], row_recv.at[0, chunks - 1]).start()

    if late_lines:
        for way, cond in ahead + behind:
            for q in range(split_by, pieces):
                pl.when(cond & late(line))(shard(q, line, pair, way, True).start)
        gather(range(split_by, pieces), True)
        bulk(CORE, 2 * late_lines, 1).wait_recv()

        @pl.loop(0, 2 * late_lines)
        def _(m):
            keep(1, whole((c * 2 * late_lines + m) * 2 + 1 - core))

    @pl.loop(0, chunks)
    def _(i):
        here = pl.ds(pl.multiple_of(i * chunk, chunk), chunk)
        out_ref[:, here] = partial(0, here)

    for h, (helper, _) in enumerate(helps):
        pl.when(r == helper)(row_tail(h, (r, 0), relay, relay, relay_send.at[0], relay_recv.at[0]).wait_send)
    bulk(PAIR, 2 * lines).wait_send()
    bulk(CORE, nr).wait_send()
    for l in range(lines):
        if l > 0:
            pl.when(line == l)(bulk(LEFT, 2 * (lines - l)).wait_send)
        if l < lines - 1:
            pl.when(line == l)(bulk(RIGHT, 2 * (l + 1)).wait_send)

    for i in range(chunks):
        here = pl.ds(i * chunk, chunk)
        total = out_ref[:, here]
        for j in range(1, nc):
            out_chunk(j, i).wait_recv()
            total = total + got[j - 1, i]
        out_ref[:, here] = total
    for j in range(1, nc):
        peer = {"device_id": (r, lax.rem(c + j, nc)), "device_id_type": MESH}
        pltpu.make_async_remote_copy(
            row_hbm, rows.at[j], row_send.at[j - 1], row_recv.at[j - 1, 0], **peer
        ).wait_send()
        pltpu.make_async_remote_copy(
            theirs.at[j - 1], got.at[j - 1], out_send.at[j - 1], out_recv.at[j - 1, 0], **peer
        ).wait_send()


def solution(mesh):
    nr, nc = mesh.shape["rows"], mesh.shape["cols"]

    def body(kernel, row_orbitals, col_orbitals, col_vectors):
        n_rows, n_cols = kernel.shape
        mb, per = row_orbitals.shape[1], col_orbitals.shape[1]
        norb = mb * nc
        nb = norb // nc
        chunks = n_rows // 256
        chunk = n_rows // chunks
        pieces = 4 if per % 32 == 0 else 2
        detour = n_rows // 1024 * 40 if nc == 2 and nr > 4 else 0
        f32, bf16, dma = jnp.float32, jnp.bfloat16, pltpu.SemaphoreType.DMA
        return pl.pallas_call(
            functools.partial(exchange_kernel, nr, nc, chunks, pieces, detour),
            out_shape=pltpu.VMEM((nb, n_rows), f32),
            in_specs=[pl.BlockSpec(memory_space=pl.ANY)] * 4,
            out_specs=pl.BlockSpec(memory_space=pltpu.VMEM),
            scratch_shapes=[
                pltpu.VMEM((n_rows, n_cols), f32),
                pltpu.VMEM((nc, n_rows, mb), f32),
                pltpu.VMEM((norb, n_cols), f32),
                pltpu.VMEM((norb, n_cols), f32),
                pltpu.VMEM((norb, n_cols), bf16),
                pltpu.VMEM((norb, n_cols), bf16),
                pltpu.VMEM((norb, n_cols), bf16),
                pltpu.VMEM((norb, n_cols), bf16),
                pltpu.VMEM((n_rows, n_cols), bf16),
                pltpu.VMEM((n_rows, n_cols), bf16),
                pltpu.VMEM((nc - 1, chunks, nb, chunk), f32),
                pltpu.VMEM((nc - 1, chunks, nb, chunk), f32),
                pltpu.VMEM((max(detour, 8), mb), f32),
                dma((4,)),
                pltpu.SemaphoreType.REGULAR((4,)),
                dma((nc - 1,)),
                dma((nc - 1, chunks)),
                dma((4,)),
                dma((pieces, 2, nr // 4)),
                dma((2,)),
                dma((nc - 1,)),
                dma((nc - 1, chunks)),
                dma((1,)),
                dma((1,)),
            ],
            compiler_params=pltpu.CompilerParams(
                collective_id=0, has_side_effects=True, vmem_limit_bytes=60 * 1024 * 1024
            ),
        )(kernel, row_orbitals, col_orbitals.T, col_vectors.T)

    in_specs = (P("rows", "cols"), P("rows", "cols"), P("cols", "rows"), P("cols", "rows"))
    out_specs = P("cols", "rows")
    return jax.shard_map(body, mesh=mesh, in_specs=in_specs, out_specs=out_specs, check_vma=False)
```

```python
import functools

import jax
import jax.numpy as jnp
from jax import lax
from jax.experimental import pallas as pl
from jax.experimental.pallas import tpu as pltpu
from jax.sharding import PartitionSpec as P

MESH = pl.DeviceIdType.MESH
LEFT, RIGHT, PAIR, CORE = range(4)


def split(x):
    hi = x.astype(jnp.bfloat16)
    return hi, (x - hi.astype(jnp.float32)).astype(jnp.bfloat16)


def dot3(a_hi, a_lo, b_hi, b_lo, dims):
    dot = functools.partial(lax.dot_general, dimension_numbers=(dims, ((), ())), preferred_element_type=jnp.float32)
    return dot(a_lo, b_hi) + dot(a_hi, b_lo) + dot(a_hi, b_hi)


def exchange_kernel(
    nr, nc, chunks, pieces, helpers, detour,
    k_hbm, row_hbm, orb_hbm, vec_hbm, out_ref,
    k, rows, orb, vec, orb_hi, orb_lo, vec_hi, vec_lo, w_hi, w_lo, theirs, got, relay,
    local_sem, ready, row_send, row_recv, col_send, col_recv, core_recv, out_send, out_recv, relay_send, relay_recv,
):
    r, c = lax.axis_index("rows"), lax.axis_index("cols")
    core, chip = lax.rem(r, 2), r // 2
    pair, line, lines = lax.rem(chip, 2), chip // 2, nr // 4
    per = orb_hbm.shape[0]
    chunk = row_hbm.shape[0] // chunks
    mb = row_hbm.shape[1]
    nb = theirs.shape[2]

    def at(l, p, q):
        return (l * 2 + p) * 2 + q

    goal = {
        LEFT: at(line - 1, pair, core),
        RIGHT: at(line + 1, pair, core),
        PAIR: at(line, 1 - pair, core),
        CORE: at(line, pair, 1 - core),
    }
    has_left, has_right = line > 0, line < lines - 1

    barrier = pltpu.get_barrier_semaphore()

    def greet(row, col):
        pl.semaphore_signal(barrier, inc=1, device_id=(row, col), device_id_type=MESH)

    for j in range(1, nc):
        greet(r, lax.rem(c + j, nc))
    pl.when(core == 1)(lambda: greet(goal[CORE], c))
    pl.when(pair == 0)(lambda: greet(goal[PAIR], c))
    pl.when(has_right)(lambda: greet(goal[RIGHT], c))

    k_copy = pltpu.make_async_copy(k_hbm, k, local_sem.at[0])
    row_copy = pltpu.make_async_copy(row_hbm, rows.at[0], local_sem.at[1])
    own = pl.ds(pl.multiple_of(r * per, per), per)
    orb_copy = pltpu.make_async_copy(orb_hbm, orb.at[own], local_sem.at[2])
    vec_copy = pltpu.make_async_copy(vec_hbm, vec.at[own], local_sem.at[3])

    pl.semaphore_wait(barrier, nc - 1 + 1 - core + pair + has_left.astype(jnp.int32))

    def row_chunk(j, i, size=chunk):
        at_rows = pl.ds(i * chunk if isinstance(i, int) else pl.multiple_of(i * chunk, chunk), size)
        return pltpu.make_async_remote_copy(
            src_ref=row_hbm.at[at_rows],
            dst_ref=rows.at[j, at_rows],
            send_sem=row_send.at[j - 1],
            recv_sem=row_recv.at[j - 1, i],
            device_id=(r, lax.rem(c + j, nc)),
            device_id_type=MESH,
        )

    to_first = (r == 0) & (c == 1)
    helper = (core == 0) & (chip > 0) & (chip <= helpers)
    direct = chunk - helpers * detour

    def row_tail(h, device, src, dst, send, recv):
        there = pl.ds(pl.multiple_of((chunks - 1) * chunk + direct + h * detour, 8), detour)
        return pltpu.make_async_remote_copy(
            src_ref=relay if src is relay else src.at[there],
            dst_ref=relay if dst is relay else dst.at[1, there],
            send_sem=send,
            recv_sem=recv,
            device_id=device,
            device_id_type=MESH,
        )

    def row_across():
        return row_tail(0, (r, 0), relay, relay, relay_send.at[0], relay_recv.at[0])

    def row_round(l, p):
        h = l * 2 + p - 1
        if h < helpers:
            to = (at(l, p, 0), c)
            pl.when(to_first)(row_tail(h, to, row_hbm, relay, row_send.at[0], relay_recv.at[0]).start)

    for i in range(chunks):
        for j in range(1, nc):
            if helpers and i == chunks - 1:
                pl.when(~to_first)(row_chunk(j, i).start)
                pl.when(to_first)(row_chunk(j, i, direct).start)
            else:
                row_chunk(j, i).start()

    def answer(way, slot):
        pl.semaphore_signal(ready.at[slot], inc=1, device_id=(goal[way], c), device_id_type=MESH)

    pl.when(core == 0)(lambda: answer(CORE, CORE))
    pl.when(pair == 1)(lambda: answer(PAIR, PAIR))
    pl.when(has_left)(lambda: answer(LEFT, RIGHT))

    split_by = pieces // 2
    part = per // split_by
    late_lines = lines // nc if lines % nc == 0 else 0

    def late(l):
        return l // late_lines == c if late_lines else l < 0

    def at_piece(q, s):
        return pl.ds(pl.multiple_of(s * per + q % split_by * part, part), part)

    def shard(q, l, p, way, first=False):
        t = q // split_by
        there = (orb, vec)[t].at[at_piece(q, at(l, p, core))]
        return pltpu.make_async_remote_copy(
            src_ref=(orb_hbm, vec_hbm)[t].at[pl.ds(q % split_by * part, part)] if first else there,
            dst_ref=there,
            send_sem=col_send.at[way],
            recv_sem=core_recv.at[phase_of(q, l)] if way == CORE else col_recv.at[q, p, l],
            device_id=(goal[way], c),
            device_id_type=MESH,
        )

    def phase_of(q, l):
        return 0 if q < split_by else late(l).astype(jnp.int32)

    def line_sources(d):
        if d == 0:
            return [(line, None, ())]
        return [
            (line - d, line - d >= 0, ((RIGHT, has_right), (PAIR, None), (CORE, None))),
            (line + d, line + d < lines, ((LEFT, has_left), (PAIR, None), (CORE, None))),
        ]

    def both(a, b):
        return b if a is None else a if b is None else a & b

    def when(cond, do):
        if cond is None:
            do()
        else:
            pl.when(cond)(do)

    def keep(t, rows_here):
        if t == 0:
            orb_hi[rows_here], orb_lo[rows_here] = split(orb[rows_here])
        else:
            vec_hi[rows_here], vec_lo[rows_here] = split(-vec[rows_here])

    def whole(s):
        return pl.ds(pl.multiple_of(s * per, per), per)

    def now(q, l, second):
        if q < split_by:
            return None
        return late(l) if second else ~late(l)

    def pass_on(q, d, second):
        for l, there, ways in line_sources(d):
            def go(l=l, ways=ways):
                shard(q, l, pair, PAIR).wait_recv()
                for way, cond in ways:
                    when(cond, shard(q, l, pair, way).start)
                keep(q // split_by, at_piece(q, at(l, pair, core)))
            when(both(there, now(q, l, second)), go)

    def pass_over(q, d, second):
        for l, there, _ in line_sources(d):
            def go(l=l):
                shard(q, l, 1 - pair, PAIR).wait_recv()
                shard(q, l, 1 - pair, CORE).start()
                keep(q // split_by, at_piece(q, at(l, 1 - pair, core)))
            when(both(there, now(q, l, second)), go)

    def gather(some, second, after=lambda d: None):
        for d in range(1, lines):
            for q in some:
                pass_on(q, d, second)
            for q in some:
                pass_over(q, d - 1, second)
            after(d)
        for q in some:
            pass_over(q, lines - 1, second)

    ahead = ((LEFT, has_left), (PAIR, pair == 1), (CORE, core == 0))
    behind = ((CORE, core == 1), (PAIR, pair == 0), (RIGHT, has_right))
    for q in range(pieces):
        for way, cond in ahead:
            when(both(cond, now(q, line, False)), shard(q, line, pair, way, True).start)
    for way, cond in behind:
        pl.when(cond)(lambda way=way: pl.semaphore_wait(ready.at[way], 1))
    for q in range(pieces):
        for way, cond in behind:
            when(both(cond, now(q, line, False)), shard(q, line, pair, way, True).start)

    row_round(0, 1)
    row_round(1, 0)
    for copy in (k_copy, row_copy, orb_copy, vec_copy):
        copy.start()
    gather(range(pieces), False, lambda d: (row_round(d, 0), row_round(d - 1, 1)) if d > 1 else None)
    if helpers:

        @pl.when(helper & (c == 1))
        def _():
            row_across().wait_recv()
            row_across().start()

    def bulk(way, count, phase=0):
        some = orb.at[pl.ds(0, count * per)]
        return pltpu.make_async_remote_copy(
            src_ref=some,
            dst_ref=some,
            send_sem=col_send.at[way],
            recv_sem=core_recv.at[phase],
            device_id=(goal[CORE], c),
            device_id_type=MESH,
        )

    for copy in (orb_copy, vec_copy, k_copy, row_copy):
        copy.wait()
    for t in range(2):
        keep(t, whole(r))
    bulk(CORE, nr - 2 * late_lines).wait_recv()

    @pl.loop(0, nr // 2)
    def _(m):
        keep(0, whole(m * 2 + 1 - core))

    @pl.loop(0, nr // 2 - 2 * late_lines)
    def _(m):
        m = m + jnp.where(m >= c * 2 * late_lines, 2 * late_lines, 0)
        keep(1, whole(m * 2 + 1 - core))

    def out_chunk(j, i):
        return pltpu.make_async_remote_copy(
            src_ref=theirs.at[j - 1, i],
            dst_ref=got.at[j - 1, i],
            send_sem=out_send.at[j - 1],
            recv_sem=out_recv.at[j - 1, i],
            device_id=(r, lax.rem(c + j, nc)),
            device_id_type=MESH,
        )

    def partial(j, here):
        block = pl.ds(pl.multiple_of(lax.rem(c + j, nc) * nb, nb), nb)
        return dot3(vec_hi[block], vec_lo[block], w_hi[here], w_lo[here], ((1,), (1,)))

    @pl.loop(0, chunks)
    def _(i):
        here = pl.ds(pl.multiple_of(i * chunk, chunk), chunk)
        gram = None
        for j in range(nc):
            if j > 0:
                row_chunk(j, i).wait_recv()
            block = pl.ds(pl.multiple_of(lax.rem(c - j + nc, nc) * mb, mb), mb)
            term = dot3(*split(rows[j, here, :]), orb_hi[block], orb_lo[block], ((1,), (0,)))
            gram = term if gram is None else gram + term
        w_hi[here], w_lo[here] = split(k[here] * gram)
        for j in range(1, nc):
            theirs[j - 1, i] = partial(j, here)
            out_chunk(j, i).start()

        if late_lines:
            for way, cond in ahead + behind:
                for q in range(split_by, pieces):
                    pl.when(cond & late(line) & (i == 0))(shard(q, line, pair, way, True).start)

    if helpers:

        @pl.when(helper & (c == 0))
        def _():
            row_across().wait_recv()
            row_tail(chip - 1, (0, 0), relay, rows, relay_send.at[0], row_recv.at[0, chunks - 1]).start()

    if late_lines:
        gather(range(split_by, pieces), True)
        bulk(CORE, 2 * late_lines, 1).wait_recv()

        @pl.loop(0, 2 * late_lines)
        def _(m):
            keep(1, whole((c * 2 * late_lines + m) * 2 + 1 - core))

    @pl.loop(0, chunks)
    def _(i):
        here = pl.ds(pl.multiple_of(i * chunk, chunk), chunk)
        out_ref[:, here] = partial(0, here)

    if helpers:
        pl.when(helper)(row_across().wait_send)
    bulk(PAIR, 2 * lines).wait_send()
    bulk(CORE, nr).wait_send()
    for l in range(lines):
        if l > 0:
            pl.when(line == l)(bulk(LEFT, 2 * (lines - l)).wait_send)
        if l < lines - 1:
            pl.when(line == l)(bulk(RIGHT, 2 * (l + 1)).wait_send)

    for i in range(chunks):
        here = pl.ds(i * chunk, chunk)
        total = out_ref[:, here]
        for j in range(1, nc):
            out_chunk(j, i).wait_recv()
            total = total + got[j - 1, i]
        out_ref[:, here] = total
    for j in range(1, nc):
        peer = {"device_id": (r, lax.rem(c + j, nc)), "device_id_type": MESH}
        pltpu.make_async_remote_copy(
            row_hbm, rows.at[j], row_send.at[j - 1], row_recv.at[j - 1, 0], **peer
        ).wait_send()
        pltpu.make_async_remote_copy(
            theirs.at[j - 1], got.at[j - 1], out_send.at[j - 1], out_recv.at[j - 1, 0], **peer
        ).wait_send()


def solution(mesh):
    nr, nc = mesh.shape["rows"], mesh.shape["cols"]

    def body(kernel, row_orbitals, col_orbitals, col_vectors):
        n_rows, n_cols = kernel.shape
        mb, per = row_orbitals.shape[1], col_orbitals.shape[1]
        norb = mb * nc
        nb = norb // nc
        chunks = n_rows // 256
        chunk = n_rows // chunks
        pieces = 4 if per % 32 == 0 else 2
        helpers = min(nr // 2 - 2, 6) if nc == 2 else 0
        detour = n_rows // 64
        f32, bf16, dma = jnp.float32, jnp.bfloat16, pltpu.SemaphoreType.DMA
        return pl.pallas_call(
            functools.partial(exchange_kernel, nr, nc, chunks, pieces, helpers, detour),
            out_shape=pltpu.VMEM((nb, n_rows), f32),
            in_specs=[pl.BlockSpec(memory_space=pl.ANY)] * 4,
            out_specs=pl.BlockSpec(memory_space=pltpu.VMEM),
            scratch_shapes=[
                pltpu.VMEM((n_rows, n_cols), f32),
                pltpu.VMEM((nc, n_rows, mb), f32),
                pltpu.VMEM((norb, n_cols), f32),
                pltpu.VMEM((norb, n_cols), f32),
                pltpu.VMEM((norb, n_cols), bf16),
                pltpu.VMEM((norb, n_cols), bf16),
                pltpu.VMEM((norb, n_cols), bf16),
                pltpu.VMEM((norb, n_cols), bf16),
                pltpu.VMEM((n_rows, n_cols), bf16),
                pltpu.VMEM((n_rows, n_cols), bf16),
                pltpu.VMEM((nc - 1, chunks, nb, chunk), f32),
                pltpu.VMEM((nc - 1, chunks, nb, chunk), f32),
                pltpu.VMEM((detour, mb), f32),
                dma((4,)),
                pltpu.SemaphoreType.REGULAR((4,)),
                dma((nc - 1,)),
                dma((nc - 1, chunks)),
                dma((4,)),
                dma((pieces, 2, nr // 4)),
                dma((2,)),
                dma((nc - 1,)),
                dma((nc - 1, chunks)),
                dma((1,)),
                dma((1,)),
            ],
            compiler_params=pltpu.CompilerParams(
                collective_id=0, has_side_effects=True, vmem_limit_bytes=60 * 1024 * 1024
            ),
        )(kernel, row_orbitals, col_orbitals.T, col_vectors.T)

    in_specs = (P("rows", "cols"), P("rows", "cols"), P("cols", "rows"), P("cols", "rows"))
    out_specs = P("cols", "rows")
    return jax.shard_map(body, mesh=mesh, in_specs=in_specs, out_specs=out_specs, check_vma=False)
```

```python
import functools

import jax
import jax.numpy as jnp
from jax import lax
from jax.experimental import pallas as pl
from jax.experimental.pallas import tpu as pltpu
from jax.sharding import PartitionSpec as P

MESH = pl.DeviceIdType.MESH
LEFT, RIGHT, PAIR, CORE = range(4)


def split(x):
    hi = x.astype(jnp.bfloat16)
    return hi, (x - hi.astype(jnp.float32)).astype(jnp.bfloat16)


def dot3(a_hi, a_lo, b_hi, b_lo, dims):
    dot = functools.partial(lax.dot_general, dimension_numbers=(dims, ((), ())), preferred_element_type=jnp.float32)
    return dot(a_lo, b_hi) + dot(a_hi, b_lo) + dot(a_hi, b_hi)


def exchange_kernel(
    nr, nc, chunks, pieces, helpers, detour,
    k_hbm, row_hbm, orb_hbm, vec_hbm, out_ref,
    k, rows, orb, vec, orb_hi, orb_lo, vec_hi, vec_lo, w_hi, w_lo, theirs, got, relay,
    local_sem, ready, row_send, row_recv, col_send, col_recv, core_recv, out_send, out_recv, relay_send, relay_recv,
):
    r, c = lax.axis_index("rows"), lax.axis_index("cols")
    core, chip = lax.rem(r, 2), r // 2
    pair, line, lines = lax.rem(chip, 2), chip // 2, nr // 4
    per = orb_hbm.shape[0]
    chunk = row_hbm.shape[0] // chunks
    mb = row_hbm.shape[1]
    nb = theirs.shape[2]

    def at(l, p, q):
        return (l * 2 + p) * 2 + q

    goal = {
        LEFT: at(line - 1, pair, core),
        RIGHT: at(line + 1, pair, core),
        PAIR: at(line, 1 - pair, core),
        CORE: at(line, pair, 1 - core),
    }
    has_left, has_right = line > 0, line < lines - 1

    barrier = pltpu.get_barrier_semaphore()

    def greet(row, col):
        pl.semaphore_signal(barrier, inc=1, device_id=(row, col), device_id_type=MESH)

    for j in range(1, nc):
        greet(r, lax.rem(c + j, nc))
    pl.when(core == 1)(lambda: greet(goal[CORE], c))
    pl.when(pair == 0)(lambda: greet(goal[PAIR], c))
    pl.when(has_right)(lambda: greet(goal[RIGHT], c))

    k_copy = pltpu.make_async_copy(k_hbm, k, local_sem.at[0])
    row_copy = pltpu.make_async_copy(row_hbm, rows.at[0], local_sem.at[1])
    own = pl.ds(pl.multiple_of(r * per, per), per)
    orb_copy = pltpu.make_async_copy(orb_hbm, orb.at[own], local_sem.at[2])
    vec_copy = pltpu.make_async_copy(vec_hbm, vec.at[own], local_sem.at[3])

    pl.semaphore_wait(barrier, nc - 1 + 1 - core + pair + has_left.astype(jnp.int32))

    def row_chunk(j, i, size=chunk):
        at_rows = pl.ds(i * chunk if isinstance(i, int) else pl.multiple_of(i * chunk, chunk), size)
        return pltpu.make_async_remote_copy(
            src_ref=row_hbm.at[at_rows],
            dst_ref=rows.at[j, at_rows],
            send_sem=row_send.at[j - 1],
            recv_sem=row_recv.at[j - 1, i],
            device_id=(r, lax.rem(c + j, nc)),
            device_id_type=MESH,
        )

    first = r == 0
    helper = (core == 0) & (chip > 0) & (chip <= helpers)
    direct = chunk - helpers * detour
    TO, ACROSS, BACK = range(3)

    def row_round(leg, h, device):
        there = pl.ds(pl.multiple_of((chunks - 1) * chunk + direct + h * detour, 8), detour)
        return pltpu.make_async_remote_copy(
            src_ref=row_hbm.at[there] if leg == TO else relay.at[leg - 1],
            dst_ref=rows.at[1, there] if leg == BACK else relay.at[leg],
            send_sem=row_send.at[0] if leg == TO else relay_send.at[leg - 1],
            recv_sem=row_recv.at[0, chunks - 1] if leg == BACK else relay_recv.at[leg],
            device_id=device,
            device_id_type=MESH,
        )

    def row_out(l, p):
        h = l * 2 + p - 1
        if h < helpers:
            pl.when(first)(row_round(TO, h, (at(l, p, 0), c)).start)

    for i in range(chunks):
        for j in range(1, nc):
            if helpers and i == chunks - 1:
                pl.when(~first)(row_chunk(j, i).start)
                pl.when(first)(row_chunk(j, i, direct).start)
            else:
                row_chunk(j, i).start()

    def answer(way, slot):
        pl.semaphore_signal(ready.at[slot], inc=1, device_id=(goal[way], c), device_id_type=MESH)

    pl.when(core == 0)(lambda: answer(CORE, CORE))
    pl.when(pair == 1)(lambda: answer(PAIR, PAIR))
    pl.when(has_left)(lambda: answer(LEFT, RIGHT))

    split_by = pieces // 2
    part = per // split_by
    late_lines = lines // nc if lines % nc == 0 else 0

    def late(l):
        return l // late_lines == c if late_lines else l < 0

    def at_piece(q, s):
        return pl.ds(pl.multiple_of(s * per + q % split_by * part, part), part)

    def shard(q, l, p, way, first=False):
        t = q // split_by
        there = (orb, vec)[t].at[at_piece(q, at(l, p, core))]
        return pltpu.make_async_remote_copy(
            src_ref=(orb_hbm, vec_hbm)[t].at[pl.ds(q % split_by * part, part)] if first else there,
            dst_ref=there,
            send_sem=col_send.at[way],
            recv_sem=core_recv.at[phase_of(q, l)] if way == CORE else col_recv.at[q, p, l],
            device_id=(goal[way], c),
            device_id_type=MESH,
        )

    def phase_of(q, l):
        return 0 if q < split_by else late(l).astype(jnp.int32)

    def line_sources(d):
        if d == 0:
            return [(line, None, ())]
        return [
            (line - d, line - d >= 0, ((RIGHT, has_right), (PAIR, None), (CORE, None))),
            (line + d, line + d < lines, ((LEFT, has_left), (PAIR, None), (CORE, None))),
        ]

    def both(a, b):
        return b if a is None else a if b is None else a & b

    def when(cond, do):
        if cond is None:
            do()
        else:
            pl.when(cond)(do)

    def keep(t, rows_here):
        if t == 0:
            orb_hi[rows_here], orb_lo[rows_here] = split(orb[rows_here])
        else:
            vec_hi[rows_here], vec_lo[rows_here] = split(-vec[rows_here])

    def whole(s):
        return pl.ds(pl.multiple_of(s * per, per), per)

    def now(q, l, second):
        if q < split_by:
            return None
        return late(l) if second else ~late(l)

    def pass_on(q, d, second):
        for l, there, ways in line_sources(d):
            def go(l=l, ways=ways):
                shard(q, l, pair, PAIR).wait_recv()
                for way, cond in ways:
                    when(cond, shard(q, l, pair, way).start)
                keep(q // split_by, at_piece(q, at(l, pair, core)))
            when(both(there, now(q, l, second)), go)

    def pass_over(q, d, second):
        for l, there, _ in line_sources(d):
            def go(l=l):
                shard(q, l, 1 - pair, PAIR).wait_recv()
                shard(q, l, 1 - pair, CORE).start()
                keep(q // split_by, at_piece(q, at(l, 1 - pair, core)))
            when(both(there, now(q, l, second)), go)

    def gather(some, second, after=lambda d: None):
        for d in range(1, lines):
            for q in some:
                pass_on(q, d, second)
            for q in some:
                pass_over(q, d - 1, second)
            after(d)
        for q in some:
            pass_over(q, lines - 1, second)

    ahead = ((LEFT, has_left), (PAIR, pair == 1), (CORE, core == 0))
    behind = ((CORE, core == 1), (PAIR, pair == 0), (RIGHT, has_right))
    for q in range(pieces):
        for way, cond in ahead:
            when(both(cond, now(q, line, False)), shard(q, line, pair, way, True).start)
    for way, cond in behind:
        pl.when(cond)(lambda way=way: pl.semaphore_wait(ready.at[way], 1))
    for q in range(pieces):
        for way, cond in behind:
            when(both(cond, now(q, line, False)), shard(q, line, pair, way, True).start)

    row_out(0, 1)
    row_out(1, 0)
    for copy in (k_copy, row_copy, orb_copy, vec_copy):
        copy.start()
    gather(range(pieces), False, lambda d: (row_out(d, 0), row_out(d - 1, 1)) if d > 1 else None)
    if helpers:

        @pl.when(helper)
        def _():
            row_round(TO, 0, (r, 1 - c)).wait_recv()
            row_round(ACROSS, 0, (r, 1 - c)).start()

    def bulk(way, count, phase=0):
        some = orb.at[pl.ds(0, count * per)]
        return pltpu.make_async_remote_copy(
            src_ref=some,
            dst_ref=some,
            send_sem=col_send.at[way],
            recv_sem=core_recv.at[phase],
            device_id=(goal[CORE], c),
            device_id_type=MESH,
        )

    for copy in (orb_copy, vec_copy, k_copy, row_copy):
        copy.wait()
    for t in range(2):
        keep(t, whole(r))
    bulk(CORE, nr - 2 * late_lines).wait_recv()

    @pl.loop(0, nr // 2)
    def _(m):
        keep(0, whole(m * 2 + 1 - core))

    @pl.loop(0, nr // 2 - 2 * late_lines)
    def _(m):
        m = m + jnp.where(m >= c * 2 * late_lines, 2 * late_lines, 0)
        keep(1, whole(m * 2 + 1 - core))

    def out_chunk(j, i):
        return pltpu.make_async_remote_copy(
            src_ref=theirs.at[j - 1, i],
            dst_ref=got.at[j - 1, i],
            send_sem=out_send.at[j - 1],
            recv_sem=out_recv.at[j - 1, i],
            device_id=(r, lax.rem(c + j, nc)),
            device_id_type=MESH,
        )

    def partial(j, here):
        block = pl.ds(pl.multiple_of(lax.rem(c + j, nc) * nb, nb), nb)
        return dot3(vec_hi[block], vec_lo[block], w_hi[here], w_lo[here], ((1,), (1,)))

    @pl.loop(0, chunks)
    def _(i):
        here = pl.ds(pl.multiple_of(i * chunk, chunk), chunk)
        gram = None
        for j in range(nc):
            if j > 0:
                row_chunk(j, i).wait_recv()
            block = pl.ds(pl.multiple_of(lax.rem(c - j + nc, nc) * mb, mb), mb)
            term = dot3(*split(rows[j, here, :]), orb_hi[block], orb_lo[block], ((1,), (0,)))
            gram = term if gram is None else gram + term
        w_hi[here], w_lo[here] = split(k[here] * gram)
        for j in range(1, nc):
            theirs[j - 1, i] = partial(j, here)
            out_chunk(j, i).start()

        if late_lines:
            for way, cond in ahead + behind:
                for q in range(split_by, pieces):
                    pl.when(cond & late(line) & (i == 0))(shard(q, line, pair, way, True).start)

    if helpers:

        @pl.when(helper)
        def _():
            row_round(ACROSS, 0, (r, 1 - c)).wait_recv()
            row_round(BACK, chip - 1, (0, c)).start()

    if late_lines:
        gather(range(split_by, pieces), True)
        bulk(CORE, 2 * late_lines, 1).wait_recv()

        @pl.loop(0, 2 * late_lines)
        def _(m):
            keep(1, whole((c * 2 * late_lines + m) * 2 + 1 - core))

    @pl.loop(0, chunks)
    def _(i):
        here = pl.ds(pl.multiple_of(i * chunk, chunk), chunk)
        out_ref[:, here] = partial(0, here)

    if helpers:
        for leg in (ACROSS, BACK):
            pl.when(helper)(row_round(leg, chip - 1, (0, c)).wait_send)
    bulk(PAIR, 2 * lines).wait_send()
    bulk(CORE, nr).wait_send()
    for l in range(lines):
        if l > 0:
            pl.when(line == l)(bulk(LEFT, 2 * (lines - l)).wait_send)
        if l < lines - 1:
            pl.when(line == l)(bulk(RIGHT, 2 * (l + 1)).wait_send)

    for i in range(chunks):
        here = pl.ds(i * chunk, chunk)
        total = out_ref[:, here]
        for j in range(1, nc):
            out_chunk(j, i).wait_recv()
            total = total + got[j - 1, i]
        out_ref[:, here] = total
    for j in range(1, nc):
        peer = {"device_id": (r, lax.rem(c + j, nc)), "device_id_type": MESH}
        pltpu.make_async_remote_copy(
            row_hbm, rows.at[j], row_send.at[j - 1], row_recv.at[j - 1, 0], **peer
        ).wait_send()
        pltpu.make_async_remote_copy(
            theirs.at[j - 1], got.at[j - 1], out_send.at[j - 1], out_recv.at[j - 1, 0], **peer
        ).wait_send()


def solution(mesh):
    nr, nc = mesh.shape["rows"], mesh.shape["cols"]

    def body(kernel, row_orbitals, col_orbitals, col_vectors):
        n_rows, n_cols = kernel.shape
        mb, per = row_orbitals.shape[1], col_orbitals.shape[1]
        norb = mb * nc
        nb = norb // nc
        chunks = n_rows // 256
        chunk = n_rows // chunks
        pieces = 4 if per % 32 == 0 else 2
        helpers = min(nr // 2 - 2, 6) if nc == 2 else 0
        detour = n_rows // 64
        f32, bf16, dma = jnp.float32, jnp.bfloat16, pltpu.SemaphoreType.DMA
        return pl.pallas_call(
            functools.partial(exchange_kernel, nr, nc, chunks, pieces, helpers, detour),
            out_shape=pltpu.VMEM((nb, n_rows), f32),
            in_specs=[pl.BlockSpec(memory_space=pl.ANY)] * 4,
            out_specs=pl.BlockSpec(memory_space=pltpu.VMEM),
            scratch_shapes=[
                pltpu.VMEM((n_rows, n_cols), f32),
                pltpu.VMEM((nc, n_rows, mb), f32),
                pltpu.VMEM((norb, n_cols), f32),
                pltpu.VMEM((norb, n_cols), f32),
                pltpu.VMEM((norb, n_cols), bf16),
                pltpu.VMEM((norb, n_cols), bf16),
                pltpu.VMEM((norb, n_cols), bf16),
                pltpu.VMEM((norb, n_cols), bf16),
                pltpu.VMEM((n_rows, n_cols), bf16),
                pltpu.VMEM((n_rows, n_cols), bf16),
                pltpu.VMEM((nc - 1, chunks, nb, chunk), f32),
                pltpu.VMEM((nc - 1, chunks, nb, chunk), f32),
                pltpu.VMEM((2, detour, mb), f32),
                dma((4,)),
                pltpu.SemaphoreType.REGULAR((4,)),
                dma((nc - 1,)),
                dma((nc - 1, chunks)),
                dma((4,)),
                dma((pieces, 2, nr // 4)),
                dma((2,)),
                dma((nc - 1,)),
                dma((nc - 1, chunks)),
                dma((2,)),
                dma((2,)),
            ],
            compiler_params=pltpu.CompilerParams(
                collective_id=0, has_side_effects=True, vmem_limit_bytes=60 * 1024 * 1024
            ),
        )(kernel, row_orbitals, col_orbitals.T, col_vectors.T)

    in_specs = (P("rows", "cols"), P("rows", "cols"), P("cols", "rows"), P("cols", "rows"))
    out_specs = P("cols", "rows")
    return jax.shard_map(body, mesh=mesh, in_specs=in_specs, out_specs=out_specs, check_vma=False)
```

```python
import functools

import jax
import jax.numpy as jnp
from jax import lax
from jax.experimental import pallas as pl
from jax.experimental.pallas import tpu as pltpu
from jax.sharding import PartitionSpec as P

MESH = pl.DeviceIdType.MESH
LEFT, RIGHT, PAIR, CORE = range(4)


def split(x):
    hi = x.astype(jnp.bfloat16)
    return hi, (x - hi.astype(jnp.float32)).astype(jnp.bfloat16)


def dot3(a_hi, a_lo, b_hi, b_lo, dims):
    dot = functools.partial(lax.dot_general, dimension_numbers=(dims, ((), ())), preferred_element_type=jnp.float32)
    return dot(a_lo, b_hi) + dot(a_hi, b_lo) + dot(a_hi, b_hi)


def exchange_kernel(
    nr, nc, chunks, pieces, helpers, detour,
    k_hbm, row_hbm, orb_hbm, vec_hbm, out_ref,
    k, rows, orb, vec, orb_hi, orb_lo, vec_hi, vec_lo, w_hi, w_lo, theirs, got, relay, lead,
    local_sem, ready, row_send, row_recv, col_send, col_recv, core_recv, out_send, out_recv, relay_send, relay_recv,
):
    r, c = lax.axis_index("rows"), lax.axis_index("cols")
    core, chip = lax.rem(r, 2), r // 2
    pair, line, lines = lax.rem(chip, 2), chip // 2, nr // 4
    per = orb_hbm.shape[0]
    chunk = row_hbm.shape[0] // chunks
    mb = row_hbm.shape[1]
    nb = theirs.shape[2]

    def at(l, p, q):
        return (l * 2 + p) * 2 + q

    goal = {
        LEFT: at(line - 1, pair, core),
        RIGHT: at(line + 1, pair, core),
        PAIR: at(line, 1 - pair, core),
        CORE: at(line, pair, 1 - core),
    }
    has_left, has_right = line > 0, line < lines - 1

    barrier = pltpu.get_barrier_semaphore()

    def greet(row, col):
        pl.semaphore_signal(barrier, inc=1, device_id=(row, col), device_id_type=MESH)

    for j in range(1, nc):
        greet(r, lax.rem(c + j, nc))
    pl.when(core == 1)(lambda: greet(goal[CORE], c))
    pl.when(pair == 0)(lambda: greet(goal[PAIR], c))
    pl.when(has_right)(lambda: greet(goal[RIGHT], c))

    k_copy = pltpu.make_async_copy(k_hbm, k, local_sem.at[0])
    row_copy = pltpu.make_async_copy(row_hbm, rows.at[0], local_sem.at[1])
    own = pl.ds(pl.multiple_of(r * per, per), per)
    orb_copy = pltpu.make_async_copy(orb_hbm, orb.at[own], local_sem.at[2])
    vec_copy = pltpu.make_async_copy(vec_hbm, vec.at[own], local_sem.at[3])

    n_lead = lead.shape[0]
    lead_copy = pltpu.make_async_copy(row_hbm.at[pl.ds(0, n_lead)], lead, local_sem.at[4])
    pl.when(c == 0)(lead_copy.start)
    pl.when(c == 0)(lead_copy.wait)
    pl.semaphore_wait(barrier, nc - 1 + 1 - core + pair + has_left.astype(jnp.int32))

    def row_lead(j):
        return pltpu.make_async_remote_copy(
            src_ref=lead,
            dst_ref=rows.at[j, pl.ds(0, n_lead)],
            send_sem=row_send.at[j - 1],
            recv_sem=row_recv.at[j - 1, 0],
            device_id=(r, lax.rem(c + j, nc)),
            device_id_type=MESH,
        )

    def row_chunk(j, i, size=chunk, skip=0):
        at_rows = pl.ds(i * chunk + skip if isinstance(i, int) else pl.multiple_of(i * chunk, chunk), size)
        return pltpu.make_async_remote_copy(
            src_ref=row_hbm.at[at_rows],
            dst_ref=rows.at[j, at_rows],
            send_sem=row_send.at[j - 1],
            recv_sem=row_recv.at[j - 1, i],
            device_id=(r, lax.rem(c + j, nc)),
            device_id_type=MESH,
        )

    first = r == 0
    helper = (core == 0) & (chip > 0) & (chip <= helpers)
    direct = chunk - helpers * detour
    TO, ACROSS, BACK = range(3)

    def row_round(leg, h, device):
        there = pl.ds(pl.multiple_of((chunks - 1) * chunk + direct + h * detour, 8), detour)
        return pltpu.make_async_remote_copy(
            src_ref=row_hbm.at[there] if leg == TO else relay.at[leg - 1],
            dst_ref=rows.at[1, there] if leg == BACK else relay.at[leg],
            send_sem=row_send.at[0] if leg == TO else relay_send.at[leg - 1],
            recv_sem=row_recv.at[0, chunks - 1] if leg == BACK else relay_recv.at[leg],
            device_id=device,
            device_id_type=MESH,
        )

    def row_out(l, p):
        h = l * 2 + p - 1
        if h < helpers:
            pl.when(first)(row_round(TO, h, (at(l, p, 0), c)).start)

    for i in range(chunks):
        for j in range(1, nc):
            if helpers and i == chunks - 1:
                pl.when(~first)(row_chunk(j, i).start)
                pl.when(first)(row_chunk(j, i, direct).start)
            elif i == 0:
                pl.when(c == 0)(row_lead(j).start)
                pl.when(c == 0)(row_chunk(j, 0, chunk - n_lead, n_lead).start)
                pl.when(c > 0)(row_chunk(j, 0).start)
            else:
                row_chunk(j, i).start()

    def answer(way, slot):
        pl.semaphore_signal(ready.at[slot], inc=1, device_id=(goal[way], c), device_id_type=MESH)

    pl.when(core == 0)(lambda: answer(CORE, CORE))
    pl.when(pair == 1)(lambda: answer(PAIR, PAIR))
    pl.when(has_left)(lambda: answer(LEFT, RIGHT))

    split_by = pieces // 2
    part = per // split_by
    late_lines = lines // nc if lines % nc == 0 else 0

    def late(l):
        return l // late_lines == c if late_lines else l < 0

    def at_piece(q, s):
        return pl.ds(pl.multiple_of(s * per + q % split_by * part, part), part)

    def shard(q, l, p, way, first=False):
        t = q // split_by
        there = (orb, vec)[t].at[at_piece(q, at(l, p, core))]
        return pltpu.make_async_remote_copy(
            src_ref=(orb_hbm, vec_hbm)[t].at[pl.ds(q % split_by * part, part)] if first else there,
            dst_ref=there,
            send_sem=col_send.at[way],
            recv_sem=core_recv.at[phase_of(q, l)] if way == CORE else col_recv.at[q, p, l],
            device_id=(goal[way], c),
            device_id_type=MESH,
        )

    def phase_of(q, l):
        return 0 if q < split_by else late(l).astype(jnp.int32)

    def line_sources(d):
        if d == 0:
            return [(line, None, ())]
        return [
            (line - d, line - d >= 0, ((RIGHT, has_right), (PAIR, None), (CORE, None))),
            (line + d, line + d < lines, ((LEFT, has_left), (PAIR, None), (CORE, None))),
        ]

    def both(a, b):
        return b if a is None else a if b is None else a & b

    def when(cond, do):
        if cond is None:
            do()
        else:
            pl.when(cond)(do)

    def keep(t, rows_here):
        if t == 0:
            orb_hi[rows_here], orb_lo[rows_here] = split(orb[rows_here])
        else:
            vec_hi[rows_here], vec_lo[rows_here] = split(-vec[rows_here])

    def whole(s):
        return pl.ds(pl.multiple_of(s * per, per), per)

    def now(q, l, second):
        if q < split_by:
            return None
        return late(l) if second else ~late(l)

    def pass_on(q, d, second):
        for l, there, ways in line_sources(d):
            def go(l=l, ways=ways):
                shard(q, l, pair, PAIR).wait_recv()
                for way, cond in ways:
                    when(cond, shard(q, l, pair, way).start)
                keep(q // split_by, at_piece(q, at(l, pair, core)))
            when(both(there, now(q, l, second)), go)

    def pass_over(q, d, second):
        for l, there, _ in line_sources(d):
            def go(l=l):
                shard(q, l, 1 - pair, PAIR).wait_recv()
                shard(q, l, 1 - pair, CORE).start()
                keep(q // split_by, at_piece(q, at(l, 1 - pair, core)))
            when(both(there, now(q, l, second)), go)

    def gather(some, second, after=lambda d: None):
        for d in range(1, lines):
            for q in some:
                pass_on(q, d, second)
            for q in some:
                pass_over(q, d - 1, second)
            after(d)
        for q in some:
            pass_over(q, lines - 1, second)

    ahead = ((LEFT, has_left), (PAIR, pair == 1), (CORE, core == 0))
    behind = ((CORE, core == 1), (PAIR, pair == 0), (RIGHT, has_right))
    for q in range(pieces):
        for way, cond in ahead:
            when(both(cond, now(q, line, False)), shard(q, line, pair, way, True).start)
    for way, cond in behind:
        pl.when(cond)(lambda way=way: pl.semaphore_wait(ready.at[way], 1))
    for q in range(pieces):
        for way, cond in behind:
            when(both(cond, now(q, line, False)), shard(q, line, pair, way, True).start)

    row_out(0, 1)
    row_out(1, 0)
    for copy in (k_copy, row_copy, orb_copy, vec_copy):
        copy.start()
    gather(range(pieces), False, lambda d: (row_out(d, 0), row_out(d - 1, 1)) if d > 1 else None)
    if helpers:

        @pl.when(helper)
        def _():
            row_round(TO, 0, (r, 1 - c)).wait_recv()
            row_round(ACROSS, 0, (r, 1 - c)).start()

    def bulk(way, count, phase=0):
        some = orb.at[pl.ds(0, count * per)]
        return pltpu.make_async_remote_copy(
            src_ref=some,
            dst_ref=some,
            send_sem=col_send.at[way],
            recv_sem=core_recv.at[phase],
            device_id=(goal[CORE], c),
            device_id_type=MESH,
        )

    for copy in (orb_copy, vec_copy, k_copy, row_copy):
        copy.wait()
    for t in range(2):
        keep(t, whole(r))
    bulk(CORE, nr - 2 * late_lines).wait_recv()

    @pl.loop(0, nr // 2)
    def _(m):
        keep(0, whole(m * 2 + 1 - core))

    @pl.loop(0, nr // 2 - 2 * late_lines)
    def _(m):
        m = m + jnp.where(m >= c * 2 * late_lines, 2 * late_lines, 0)
        keep(1, whole(m * 2 + 1 - core))

    def out_chunk(j, i):
        return pltpu.make_async_remote_copy(
            src_ref=theirs.at[j - 1, i],
            dst_ref=got.at[j - 1, i],
            send_sem=out_send.at[j - 1],
            recv_sem=out_recv.at[j - 1, i],
            device_id=(r, lax.rem(c + j, nc)),
            device_id_type=MESH,
        )

    def partial(j, here):
        block = pl.ds(pl.multiple_of(lax.rem(c + j, nc) * nb, nb), nb)
        return dot3(vec_hi[block], vec_lo[block], w_hi[here], w_lo[here], ((1,), (1,)))

    @pl.loop(0, chunks)
    def _(i):
        here = pl.ds(pl.multiple_of(i * chunk, chunk), chunk)
        gram = None
        for j in range(nc):
            if j > 0:
                row_chunk(j, i).wait_recv()
            block = pl.ds(pl.multiple_of(lax.rem(c - j + nc, nc) * mb, mb), mb)
            term = dot3(*split(rows[j, here, :]), orb_hi[block], orb_lo[block], ((1,), (0,)))
            gram = term if gram is None else gram + term
        w_hi[here], w_lo[here] = split(k[here] * gram)
        for j in range(1, nc):
            theirs[j - 1, i] = partial(j, here)
            out_chunk(j, i).start()

        if late_lines:
            for way, cond in ahead + behind:
                for q in range(split_by, pieces):
                    pl.when(cond & late(line) & (i == 0))(shard(q, line, pair, way, True).start)

    if helpers:

        @pl.when(helper)
        def _():
            row_round(ACROSS, 0, (r, 1 - c)).wait_recv()
            row_round(BACK, chip - 1, (0, c)).start()

    if late_lines:
        gather(range(split_by, pieces), True)
        bulk(CORE, 2 * late_lines, 1).wait_recv()

        @pl.loop(0, 2 * late_lines)
        def _(m):
            keep(1, whole((c * 2 * late_lines + m) * 2 + 1 - core))

    @pl.loop(0, chunks)
    def _(i):
        here = pl.ds(pl.multiple_of(i * chunk, chunk), chunk)
        out_ref[:, here] = partial(0, here)

    if helpers:
        for leg in (ACROSS, BACK):
            pl.when(helper)(row_round(leg, chip - 1, (0, c)).wait_send)
    bulk(PAIR, 2 * lines).wait_send()
    bulk(CORE, nr).wait_send()
    for l in range(lines):
        if l > 0:
            pl.when(line == l)(bulk(LEFT, 2 * (lines - l)).wait_send)
        if l < lines - 1:
            pl.when(line == l)(bulk(RIGHT, 2 * (l + 1)).wait_send)

    for i in range(chunks):
        here = pl.ds(i * chunk, chunk)
        total = out_ref[:, here]
        for j in range(1, nc):
            out_chunk(j, i).wait_recv()
            total = total + got[j - 1, i]
        out_ref[:, here] = total
    for j in range(1, nc):
        peer = {"device_id": (r, lax.rem(c + j, nc)), "device_id_type": MESH}
        pltpu.make_async_remote_copy(
            row_hbm, rows.at[j], row_send.at[j - 1], row_recv.at[j - 1, 0], **peer
        ).wait_send()
        pltpu.make_async_remote_copy(
            theirs.at[j - 1], got.at[j - 1], out_send.at[j - 1], out_recv.at[j - 1, 0], **peer
        ).wait_send()


def solution(mesh):
    nr, nc = mesh.shape["rows"], mesh.shape["cols"]

    def body(kernel, row_orbitals, col_orbitals, col_vectors):
        n_rows, n_cols = kernel.shape
        mb, per = row_orbitals.shape[1], col_orbitals.shape[1]
        norb = mb * nc
        nb = norb // nc
        chunks = n_rows // 256
        chunk = n_rows // chunks
        pieces = 4 if per % 32 == 0 else 2
        helpers = min(nr // 2 - 2, 6) if nc == 2 else 0
        detour = n_rows // 64
        f32, bf16, dma = jnp.float32, jnp.bfloat16, pltpu.SemaphoreType.DMA
        return pl.pallas_call(
            functools.partial(exchange_kernel, nr, nc, chunks, pieces, helpers, detour),
            out_shape=pltpu.VMEM((nb, n_rows), f32),
            in_specs=[pl.BlockSpec(memory_space=pl.ANY)] * 4,
            out_specs=pl.BlockSpec(memory_space=pltpu.VMEM),
            scratch_shapes=[
                pltpu.VMEM((n_rows, n_cols), f32),
                pltpu.VMEM((nc, n_rows, mb), f32),
                pltpu.VMEM((norb, n_cols), f32),
                pltpu.VMEM((norb, n_cols), f32),
                pltpu.VMEM((norb, n_cols), bf16),
                pltpu.VMEM((norb, n_cols), bf16),
                pltpu.VMEM((norb, n_cols), bf16),
                pltpu.VMEM((norb, n_cols), bf16),
                pltpu.VMEM((n_rows, n_cols), bf16),
                pltpu.VMEM((n_rows, n_cols), bf16),
                pltpu.VMEM((nc - 1, chunks, nb, chunk), f32),
                pltpu.VMEM((nc - 1, chunks, nb, chunk), f32),
                pltpu.VMEM((2, detour, mb), f32),
                pltpu.VMEM((chunk // 4, mb), f32),
                dma((5,)),
                pltpu.SemaphoreType.REGULAR((4,)),
                dma((nc - 1,)),
                dma((nc - 1, chunks)),
                dma((4,)),
                dma((pieces, 2, nr // 4)),
                dma((2,)),
                dma((nc - 1,)),
                dma((nc - 1, chunks)),
                dma((2,)),
                dma((2,)),
            ],
            compiler_params=pltpu.CompilerParams(
                collective_id=0, has_side_effects=True, vmem_limit_bytes=60 * 1024 * 1024
            ),
        )(kernel, row_orbitals, col_orbitals.T, col_vectors.T)

    in_specs = (P("rows", "cols"), P("rows", "cols"), P("cols", "rows"), P("cols", "rows"))
    out_specs = P("cols", "rows")
    return jax.shard_map(body, mesh=mesh, in_specs=in_specs, out_specs=out_specs, check_vma=False)
```
